256 devices in a mesh: group: 4 (over x_hi, core), tensor: 64 (over x_lo, y, z).
Axes of the slice: x: 4 (x_hi: 2, x_lo: 2; x = x_hi * 2 + x_lo), y: 4, z: 8, core: 2. Of those that a mesh axis runs over, the one named last changes fastest.
Arguments:
- hidden_in: bfloat16 [8192, 2048], P('tensor'), may hold values from -6 to 6
- queries: bfloat16 [8192, 3072], P('tensor', 'group'), may hold values from -10 to 10
- suffix_latent: bfloat16 [8192, 576], P('tensor'), may hold values from -10 to 10
- prefix_latent: bfloat16 [2048, 576], P(('group', 'tensor')), may hold values from -6 to 6
- key_up: bfloat16 [16, 128, 512], P('group'), may hold values from -0.5 to 0.5
- value_up: bfloat16 [16, 512, 128], P('group'), may hold values from -0.25 to 0.25
- output_weight: bfloat16 [2048, 2048], P('group'), may hold values from -0.125 to 0.125
- norm_gain: bfloat16 [2048], replicated, may hold values from 0.5 to 1.5
- router: bfloat16 [2048, 64], replicated, may hold values from -0.125 to 0.125
- expert_gate: bfloat16 [64, 2048, 1408], P('tensor', None, 'group'), may hold values from -0.125 to 0.125
- expert_up: bfloat16 [64, 2048, 1408], P('tensor', None, 'group'), may hold values from -0.125 to 0.125
- expert_down: bfloat16 [64, 1408, 2048], P('tensor', 'group'), may hold values from -0.15625 to 0.15625
- next_gain: bfloat16 [2048], replicated, may hold values from 0.5 to 1.5
- next_query_weight: bfloat16 [2048, 3072], P(None, 'group'), may hold values from -0.125 to 0.125
- next_latent_weight: bfloat16 [2048, 576], P(None, 'group'), may hold values from -0.125 to 0.125
- suffix_lengths: int32 [32], replicated, may hold values from 1 to 513, 8192 in all
- request_tenant: int32 [32], replicated, may hold values from 0 to 3
- tenant_lengths: int32 [4], replicated, may hold values from 1 to 1024, 2048 in all
- page_table: int32 [256], replicated, may hold values from 0 to 255, each once
- routes: int32 [4, 2048, 6], P(None, 'tensor'), may hold values from 0 to 63, all different within a row; in each aligned block of 32 rows (0 to 31, 32 to 63, ..., all dimensions but the last counted through in order) at most 4 rows name the same one
Outputs:
- layer_out: bfloat16 [2048, 4, 2048], P('tensor', 'group')
- next_queries: bfloat16 [8192, 3072], P('tensor', 'group')
- next_latent: bfloat16 [8192, 576], P('tensor', 'group')
The draws below stay inside these ranges and needn't reach their ends.
Inputs may be any that keep to these rules, and one draw needn't show every extreme that they name: `page_table`: each stored page maps to a different logical page. In each aligned block of 32 rows of routes (in its order g, a) an expert is named by at most 4 rows, and some block reaches 4; the 6 experts of a token differ.
All inputs are finite; a program needn't handle non-finite values.
Results may differ from the reference program's by a relative error of at most 0.018.
Values may be sent and summed in bfloat16 or wider, within the bound.
A program may use at most 128 MiB of HBM per device.

```python
import math
import jax
import jax.numpy as jnp
import numpy as np
from jax import lax

D = 2048
HEADS = 16
NOPE = 128
ROPE = 64
VD = 128
LAT = 512
FF_E = 1408
TOP = 6
EXPERTS = 64
TOK_T = 128
TOKENS = 8192
TOK_Q = 32
PREFIX = 2048
PAGE = 8
PAGES = 256
TENANTS = 4
REACH = 4
MAXLEN = 513
REQS = 32
CAP = 4
N_GROUP = 4
N_TENSOR = 64


def draw_queries(key, part):
    base_key = jax.random.fold_in(key, 101)
    values = jnp.clip(2.0 * jax.random.normal(base_key, (TOKENS, HEADS, NOPE + ROPE), jnp.float32), -8.0, 8.0)
    return values.reshape(TOKENS, HEADS * (NOPE + ROPE)).astype(jnp.bfloat16)


def draw_suffix_latent(key, part):
    base_key = jax.random.fold_in(key, 202)
    values = jnp.clip(jax.random.normal(base_key, (TOKENS, LAT + ROPE), jnp.float32), -6.0, 6.0)
    return values.astype(jnp.bfloat16)


def set_ends(array, rng, low, top_value):
    spot = [jax.random.randint(jax.random.fold_in(rng, axis), (), 0, length) for axis, length in enumerate(array.shape)]
    widest = array.shape.index(max(array.shape))
    next_to = spot[:widest] + [(spot[widest] + 1) % array.shape[widest]] + spot[widest + 1:]
    return array.at[tuple(spot)].set(low).at[tuple(next_to)].set(top_value)


def steps_of(key, shape, split, low, largest):
    level = 1.0
    for position, parts in split:
        heights = jax.random.uniform(jax.random.fold_in(jax.random.fold_in(key, 6), position), (parts,), jnp.float32, low / len(split), largest / len(split))
        level = level * jnp.repeat(jnp.exp(heights), shape[position] // parts).reshape((-1,) + (1,) * (len(shape) - 1 - position))
    return level


def split_up(count, total, bound, lean):
    portions = [(1 << 20) // math.isqrt(rank ** lean) + 1 for rank in range(2, count + 1)]
    surplus, counts = total - bound - (count - 1), [1] * (count - 1)
    while surplus > 0:
        free = [i for i in range(count - 1) if counts[i] < bound]
        pool, budget = sum([portions[i] for i in free]), surplus
        for i in free:
            extra = min(bound - counts[i], max(1, budget * portions[i] // pool), surplus)
            counts[i] = counts[i] + extra
            surplus = surplus - extra
    return np.array([bound] + counts)


def uneven_parts(own_key, amount, total, limit, slope):
    if amount == 2:
        one = jax.random.randint(own_key, (), max(1, total - limit), min(limit, total - 1) + 1)
        return jnp.stack([one, total - one])
    tallies = jnp.asarray(split_up(amount, total, limit, slope), jnp.int32)
    pairs = (amount - 1) // 2
    donor, receiver = tallies[1:1 + 2 * pairs:2], tallies[2:2 + 2 * pairs:2]
    slack = jnp.minimum(donor - 1, limit - receiver)
    moved = jax.random.randint(jax.random.fold_in(own_key, 1), (pairs,), 0, 1 << 20) % (slack + 1)
    tallies = tallies.at[1:1 + 2 * pairs:2].set(donor - moved).at[2:2 + 2 * pairs:2].set(receiver + moved)
    return tallies[jax.random.permutation(jax.random.fold_in(own_key, 2), amount)]


def deal_out(stream_key, own, number, rows, amount, top, reach, skew):
    order = jax.random.permutation(stream_key, amount)
    crowded, usual = shares(amount, rows * top, reach, skew, True), shares(amount, rows * top, reach, skew, False)
    places = jnp.arange(amount)

    def named(lengths, turn):
        used = int((lengths > 0).sum())
        fixed = max(1, used // 4)
        shifted = fixed + (places - fixed + turn * (used - fixed)) % max(1, amount - fixed)
        return jnp.zeros((amount,), jnp.int32).at[order[jnp.where(places < fixed, places, shifted)]].set(jnp.asarray(lengths, jnp.int32))

    lengths = jnp.where(number % 4 == 0, named(crowded, number // 4), named(usual, number - number // 4 - 1))
    mixed = jax.random.permutation(jax.random.fold_in(own, 3), amount)
    donor, receiver = mixed[0:amount // 2 * 2:2], mixed[1:amount // 2 * 2:2]
    room = jnp.minimum(lengths[donor] - 1, reach - lengths[receiver]) // 2
    room = jnp.where((donor == order[0]) | (receiver == order[0]) | (lengths[receiver] == 0), 0, jnp.maximum(room, 0))
    shifted = jax.random.randint(jax.random.fold_in(own, 4), (amount // 2,), 0, 1 << 20) % (room + 1)
    lengths = lengths.at[donor].add(-shifted).at[receiver].add(shifted)
    items = jnp.searchsorted(jnp.cumsum(lengths), jnp.arange(rows * top), side="right").astype(jnp.int32)
    listing = items.reshape(top, rows).T
    listing = listing[jax.random.permutation(jax.random.fold_in(own, 1), rows)]
    turn = jax.random.randint(jax.random.fold_in(own, 2), (rows, 1), 0, top)
    return jnp.take_along_axis(listing, (jnp.arange(top)[None, :] + turn) % top, axis=1)


def shares(amount, total, limit, skew, full):
    weights = [(1 << 20) // math.isqrt(grade ** skew) + 1 for grade in range(1, amount + 1)]
    largest = limit if full else min(limit, max(-(-total // amount), total * weights[0] // sum(weights)))
    least = 1 if total - largest >= amount - 1 else 0
    counts, spare = [largest] + [least] * (amount - 1), total - largest - least * (amount - 1)
    while spare > 0:
        movable = [i for i in range(1, amount) if counts[i] < largest] or [i for i in range(1, amount) if counts[i] < limit]
        mass, left = sum([weights[i] for i in movable]), spare
        for i in movable:
            more = min(limit - counts[i], max(1, left * weights[i] // mass), spare)
            counts[i] = counts[i] + more
            spare = spare - more
    return np.array(counts)


def normal_values(stream_key, extent, width, reach, pieces=(), kind=jnp.bfloat16):
    result = jax.random.normal(stream_key, extent, jnp.float32) * width
    if len(pieces) > 0:
        result = steps_of(stream_key, extent, pieces, -0.22, 0.18) * result
    return jnp.clip(result, min=-reach, max=reach).astype(kind)


def setup_inputs(seed: int = 0) -> dict:
    keys = jax.random.split(jax.random.key(seed), 21)
    hidden_in = normal_values(keys[0], (TOKENS, D), 1.0, 6.0, ((0, 64),))
    queries = draw_queries(jax.random.fold_in(keys[20], 71), 0)
    suffix_latent = draw_suffix_latent(jax.random.fold_in(keys[20], 71), 0)
    prefix_latent = normal_values(keys[3], (PREFIX, LAT + ROPE), 1.0, 6.0, ((0, 256),))
    key_up = normal_values(keys[4], (HEADS, NOPE, LAT), NOPE ** -0.5, 0.5, ((0, 4),))
    value_up = normal_values(keys[5], (HEADS, LAT, VD), LAT ** -0.5, 0.25, ((0, 4),))
    output_weight = normal_values(keys[6], (HEADS * VD, D), (HEADS * VD) ** -0.5, 0.125, ((0, 4),))
    norm_gain = jnp.clip(1.0 + 0.1 * jax.random.normal(keys[7], (D,), jnp.float32), 0.5, 1.5).astype(jnp.bfloat16)
    router = normal_values(keys[8], (D, EXPERTS), D ** -0.5, 0.125)
    expert_gate = normal_values(keys[9], (EXPERTS, D, FF_E), D ** -0.5, 0.125, ((0, 64), (2, 4)))
    expert_up = normal_values(keys[10], (EXPERTS, D, FF_E), D ** -0.5, 0.125, ((0, 64), (2, 4)))
    expert_down = normal_values(keys[11], (EXPERTS, FF_E, D), FF_E ** -0.5, 0.15625, ((0, 64), (1, 4)))
    next_gain = jnp.clip(1.0 + 0.1 * jax.random.normal(keys[12], (D,), jnp.float32), 0.5, 1.5).astype(jnp.bfloat16)
    next_query_weight = normal_values(keys[13], (D, HEADS * (NOPE + ROPE)), D ** -0.5, 0.125, ((1, 4),))
    next_latent_weight = normal_values(keys[14], (D, LAT + ROPE), D ** -0.5, 0.125, ((1, 4),))
    suffix_lengths = uneven_parts(keys[15], REQS, TOKENS, MAXLEN, 2).astype(jnp.int32)
    request_tenant = set_ends(jax.random.randint(keys[16], (REQS,), 0, TENANTS), jax.random.fold_in(keys[16], 1), 0, TENANTS - 1).astype(jnp.int32)
    tenant_lengths = uneven_parts(keys[17], TENANTS, PREFIX, PREFIX // 2, 1).astype(jnp.int32)
    page_table = jax.random.permutation(keys[18], PAGES).astype(jnp.int32)
    routes_keys = jax.random.split(jax.random.fold_in(keys[19], 1), N_GROUP * (TOKENS // N_GROUP) // TOK_Q)
    routes_turns = jax.random.permutation(jax.random.fold_in(keys[19], 3), N_GROUP * (TOKENS // N_GROUP) // TOK_Q)
    routes = jax.vmap(lambda own, number: deal_out(jax.random.fold_in(keys[19], 2), own, number, TOK_Q, EXPERTS, TOP, CAP, 1))(routes_keys, routes_turns).reshape((N_GROUP, TOKENS // N_GROUP, TOP))
    return {"hidden_in": hidden_in, "queries": queries, "suffix_latent": suffix_latent, "prefix_latent": prefix_latent, "key_up": key_up, "value_up": value_up, "output_weight": output_weight, "norm_gain": norm_gain, "router": router, "expert_gate": expert_gate, "expert_up": expert_up, "expert_down": expert_down, "next_gain": next_gain, "next_query_weight": next_query_weight, "next_latent_weight": next_latent_weight, "suffix_lengths": suffix_lengths, "request_tenant": request_tenant, "tenant_lengths": tenant_lengths, "page_table": page_table, "routes": routes}


VERY_NEGATIVE = -1e+30
ROUTE_SCALING = 2.446
NORM_EPSILON = 1e-06

def norm_rows(row_block, gain_vector):
    values = row_block.astype(jnp.float32)
    mean_square = lax.optimization_barrier(jnp.mean(values * values, axis=-1, keepdims=True))
    return (values * lax.rsqrt(mean_square + NORM_EPSILON) * gain_vector.astype(jnp.float32)).astype(jnp.bfloat16)

def reference(hidden_in, queries, suffix_latent, prefix_latent, key_up, value_up, output_weight, norm_gain, router, expert_gate, expert_up, expert_down, next_gain, next_query_weight, next_latent_weight, suffix_lengths, request_tenant, tenant_lengths, page_table, routes):
    token_ids = jnp.arange(TOKENS, dtype=jnp.int32)
    request_ends = jnp.cumsum(suffix_lengths).astype(jnp.int32)
    request_starts = (request_ends - suffix_lengths).astype(jnp.int32)
    request_of = lax.optimization_barrier(jnp.sum((token_ids[:, None] >= request_ends[None, :]).astype(jnp.int32), axis=1)).astype(jnp.int32)
    token_start = request_starts[request_of]
    token_tenant = request_tenant[request_of]
    tenant_ends = jnp.cumsum(tenant_lengths).astype(jnp.int32)
    tenant_starts = (tenant_ends - tenant_lengths).astype(jnp.int32)
    range_low = tenant_starts[token_tenant]
    range_high = tenant_ends[token_tenant]
    prefix_spots = jnp.arange(PREFIX, dtype=jnp.int32)
    logical = (page_table[prefix_spots // PAGE] * PAGE + prefix_spots % PAGE).astype(jnp.int32)
    padded_keys = jnp.concatenate([jnp.zeros((REACH * TOK_T, LAT + ROPE), jnp.bfloat16), suffix_latent], axis=0)
    score_scale = 1.0 / math.sqrt(NOPE + ROPE)

    def slice_attention(slice_index):
        first_token = (slice_index * TOK_T).astype(jnp.int32)
        query_block = lax.dynamic_slice_in_dim(queries, first_token, TOK_T, 0).reshape(TOK_T, HEADS, NOPE + ROPE)
        absorbed = jnp.einsum('thn,hnl->thl', query_block[:, :, :NOPE].astype(jnp.float32), key_up.astype(jnp.float32)).astype(jnp.bfloat16)
        query_full = jnp.concatenate([absorbed, query_block[:, :, NOPE:]], axis=-1)
        near_keys = lax.dynamic_slice_in_dim(padded_keys, first_token, (REACH + 1) * TOK_T, 0)
        key_rows = jnp.concatenate([prefix_latent, near_keys], axis=0)
        positions = lax.dynamic_slice_in_dim(token_ids, first_token, TOK_T, 0)
        block_start = lax.dynamic_slice_in_dim(token_start, first_token, TOK_T, 0)
        block_low = lax.dynamic_slice_in_dim(range_low, first_token, TOK_T, 0)
        block_high = lax.dynamic_slice_in_dim(range_high, first_token, TOK_T, 0)
        near_spots = first_token - REACH * TOK_T + jnp.arange((REACH + 1) * TOK_T, dtype=jnp.int32)
        near_visible = (near_spots[None, :] >= block_start[:, None]) & (near_spots[None, :] <= positions[:, None])
        far_visible = (logical[None, :] >= block_low[:, None]) & (logical[None, :] < block_high[:, None])
        visible = jnp.concatenate([far_visible, near_visible], axis=1)
        scores = jnp.einsum('thc,kc->thk', query_full.astype(jnp.float32), key_rows.astype(jnp.float32)) * score_scale
        masked = jnp.where(visible[:, None, :], scores, VERY_NEGATIVE)
        best_score = lax.optimization_barrier(jnp.max(masked, axis=-1, keepdims=True))
        weights = jnp.where(visible[:, None, :], jnp.exp(masked - best_score), 0.0)
        weight_sum = lax.optimization_barrier(jnp.sum(weights, axis=-1, keepdims=True))
        rounded = lax.optimization_barrier(weights.astype(jnp.bfloat16)).astype(jnp.float32)
        attended = jnp.einsum('thk,kl->thl', rounded, key_rows[:, :LAT].astype(jnp.float32)) / weight_sum
        latent_out = attended.astype(jnp.bfloat16)
        head_out = jnp.einsum('thl,hlv->thv', latent_out.astype(jnp.float32), value_up.astype(jnp.float32)).astype(jnp.bfloat16)
        return head_out.reshape(TOK_T, HEADS * VD)
    head_rows = lax.map(slice_attention, jnp.arange(N_TENSOR, dtype=jnp.int32)).reshape(TOKENS, HEADS * VD)
    attend_sum = jnp.dot(head_rows, output_weight, preferred_element_type=jnp.float32)
    residual = (hidden_in.astype(jnp.float32) + attend_sum).astype(jnp.bfloat16)
    normed = norm_rows(residual, norm_gain)
    route_ids = jnp.transpose(routes, (1, 0, 2)).reshape(TOKENS, TOP)
    probs = jax.nn.sigmoid(jnp.dot(normed, router, preferred_element_type=jnp.float32))
    picked = jnp.take_along_axis(probs, route_ids, axis=1)
    gate_weights = picked / lax.optimization_barrier(jnp.sum(picked, axis=1, keepdims=True)) * ROUTE_SCALING
    flat_ids = route_ids.reshape(-1)
    row_count = TOKENS * TOP
    hit_table = (flat_ids[:, None] == jnp.arange(EXPERTS, dtype=jnp.int32)[None, :]).astype(jnp.int32)
    rank_table = jnp.cumsum(hit_table, axis=0).astype(jnp.int32) - hit_table
    slot_index = lax.optimization_barrier(jnp.sum(rank_table * hit_table, axis=1)).astype(jnp.int32)
    most_rows = TOKENS // TOK_Q * CAP
    slot_rows = jnp.full((EXPERTS, most_rows), row_count, jnp.int32).at[flat_ids, slot_index].set(jnp.arange(row_count, dtype=jnp.int32))
    normed_padded = jnp.concatenate([normed, jnp.zeros((1, D), jnp.bfloat16)], axis=0)
    token_of_row = jnp.concatenate([jnp.arange(row_count, dtype=jnp.int32) // TOP, jnp.full((1,), TOKENS, jnp.int32)]).astype(jnp.int32)
    weight_of_row = jnp.concatenate([gate_weights.reshape(-1), jnp.zeros((1,), jnp.float32)])
    unit_share = FF_E // N_GROUP

    def expert_step(running, expert_index):
        rows_here = slot_rows[expert_index]
        tokens_here = token_of_row[rows_here]
        inputs = normed_padded[tokens_here]
        gate_vals = jnp.dot(inputs, expert_gate[expert_index], preferred_element_type=jnp.float32)
        up_vals = jnp.dot(inputs, expert_up[expert_index], preferred_element_type=jnp.float32)
        hidden_vals = (jax.nn.silu(gate_vals) * up_vals).astype(jnp.bfloat16)
        down_rows = expert_down[expert_index]
        combined = jnp.zeros((most_rows, D), jnp.float32)
        for quarter in range(N_GROUP):
            part_rows = jnp.dot(hidden_vals[:, quarter * unit_share:(quarter + 1) * unit_share], down_rows[quarter * unit_share:(quarter + 1) * unit_share], preferred_element_type=jnp.float32).astype(jnp.bfloat16)
            combined = combined + part_rows.astype(jnp.float32)
        running = running.at[tokens_here].add(weight_of_row[rows_here][:, None] * combined)
        return (running, None)
    moe_total, unused = lax.scan(expert_step, jnp.zeros((TOKENS + 1, D), jnp.float32), jnp.arange(EXPERTS, dtype=jnp.int32))
    layer_rows = (residual.astype(jnp.float32) + moe_total[:TOKENS]).astype(jnp.bfloat16)
    normed_next = norm_rows(layer_rows, next_gain)
    next_queries = jnp.dot(normed_next, next_query_weight, preferred_element_type=jnp.float32).astype(jnp.bfloat16)
    next_latent = jnp.dot(normed_next, next_latent_weight, preferred_element_type=jnp.float32).astype(jnp.bfloat16)
    return (layer_rows.reshape(TOKENS // N_GROUP, N_GROUP, D), next_queries, next_latent)
```

```python
import functools
import math

import jax
import jax.numpy as jnp
from jax import lax
from jax.experimental import pallas as pl
from jax.experimental.pallas import tpu as pltpu
from jax.sharding import PartitionSpec as P

NOPE = 128
ROPE = 64
LAT = 512
KEY = LAT + ROPE
PAGE = 8
REACH = 4
WIDTH = 2048
HALF = WIDTH // 2
EXPERTS = 64
TOP = 6
HEADS_DEV = 4
TOK = 128
QUARTER = 32
SLOTS = EXPERTS * 8
SCORE_SCALE = 1.0 / math.sqrt(NOPE + ROPE)
VERY_NEGATIVE = -1e30
ROUTE_SCALING = 2.446
NORM_EPSILON = 1e-06
BF16 = jnp.bfloat16
F32 = jnp.float32
MESH = pl.DeviceIdType.MESH
ANY = pl.BlockSpec(memory_space=pl.ANY)
VM = pl.BlockSpec(memory_space=pltpu.VMEM)
SM = pl.BlockSpec(memory_space=pltpu.SMEM)
DMA = pltpu.SemaphoreType.DMA
NT = (((1,), (1,)), ((), ()))
TN = (((0,), (0,)), ((), ()))


def coords():
    g = lax.axis_index("group")
    t = lax.axis_index("tensor")
    x = lax.div(g, 2) * 2 + lax.div(t, 32)
    y = lax.rem(lax.div(t, 8), 4)
    z = lax.rem(t, 8)
    return x, y, z, lax.rem(g, 2)


def group_of(x, c):
    return lax.div(x, 2) * 2 + c


def tensor_of(x, y, z):
    return (lax.rem(x, 2) * 4 + y) * 8 + z


def device(x, y, z, c):
    return {"group": group_of(x, c), "tensor": tensor_of(x, y, z)}


def remote(src, dst, send, recv, dev):
    return pltpu.make_async_remote_copy(
        src_ref=src, dst_ref=dst, send_sem=send, recv_sem=recv, device_id=dev, device_id_type=MESH
    )


def meet(peers):
    barrier = pltpu.get_barrier_semaphore()
    for peer in peers:
        pl.semaphore_signal(barrier, inc=1, device_id=peer, device_id_type=MESH)
    pl.semaphore_wait(barrier, len(peers))


def shape(dims, dtype=BF16):
    return jax.ShapeDtypeStruct(dims, dtype)


def params(cid=None, limit=56 << 20):
    if cid is None:
        return pltpu.CompilerParams(vmem_limit_bytes=limit)
    return pltpu.CompilerParams(collective_id=cid, has_side_effects=True, vmem_limit_bytes=limit)


def gather_kernel(pref, suf, pk, sk, own_sem, zs, zr, bs, br, cs, cr, us, ur, vs, vr, ws, wr):
    x, y, z, c = coords()
    g = lax.axis_index("group")
    t = lax.axis_index("tensor")
    sibling = device(x, y, z, 1 - c)
    opposite = device(lax.rem(x + 2, 4), y, z, c)
    z_dev = [None] + [device(x, y, lax.rem(z + d, 8), c) for d in range(1, 8)]
    p_dev = [None] + [
        device(lax.rem(x + d * c, 4), lax.rem(y + d * (1 - c), 4), z, c) for d in range(1, 4)
    ]
    q_dev = [None] + [
        device(lax.rem(x + d * (1 - c), 4), lax.rem(y + d * c, 4), z, c) for d in range(1, 4)
    ]
    ahead = [{"group": g, "tensor": lax.rem(t + k, 64)} for k in range(1, REACH + 1)]
    behind = [{"group": g, "tensor": lax.rem(t + 64 - k, 64)} for k in range(1, REACH + 1)]
    meet(z_dev[1:] + p_dev[1:] + q_dev[1:] + [sibling] + ahead + behind)

    def block(dp, dq, core):
        bx = lax.rem(x + 8 - dp * core - dq * (1 - core), 4)
        by = lax.rem(y + 8 - dp * (1 - core) - dq * core, 4)
        return pk.at[pl.ds(group_of(bx, core) * 64 + tensor_of(bx, by, 0), 8)]

    sends = []

    def go(src, dst, send, recv, dev):
        copy = remote(src, dst, send, recv, dev)
        copy.start()
        sends.append(copy)

    me = g * 64 + t
    own = pltpu.make_async_copy(pref, pk.at[me], own_sem)
    own.start()
    for d in range(1, 8):
        go(pref, pk.at[me], zs.at[d], zr.at[d], z_dev[d])
    for k in range(REACH):
        go(suf.at[g], sk.at[k, g], us.at[k], ur.at[k], ahead[k])
    own.wait()
    base = me - z
    for d in range(1, 8):
        row = pk.at[base + lax.rem(z + 8 - d, 8)]
        remote(pref, row, zs.at[d], zr.at[d], z_dev[d]).wait_recv()
    first = block(0, 0, c)
    for d in range(1, 4):
        go(first, first, bs.at[d, 0], br.at[d, 0], p_dev[d])
    for d in range(1, 4):
        go(first, first, bs.at[0, d], br.at[0, d], q_dev[d])
    go(first, first, cs.at[0, 0], cr.at[0, 0], sibling)
    for dp in range(1, 4):
        here = block(dp, 0, c)
        remote(here, here, bs.at[dp, 0], br.at[dp, 0], sibling).wait_recv()
        for d in range(1, 4):
            go(here, here, bs.at[dp, d], br.at[dp, d], q_dev[d])
        go(here, here, cs.at[dp, 0], cr.at[dp, 0], sibling)
    for k in range(REACH):
        here = sk.at[k, g]
        remote(here, here, us.at[k], ur.at[k], sibling).wait_recv()
        go(here, here, vs.at[k], vr.at[k], opposite)
        go(here, here, ws.at[k, 0], wr.at[k, 0], sibling)
    for dp in range(4):
        for dq in range(1, 4):
            here = block(dp, dq, c)
            remote(here, here, bs.at[dp, dq], br.at[dp, dq], sibling).wait_recv()
            go(here, here, cs.at[dp, dq], cr.at[dp, dq], sibling)
    far = lax.rem(g + 2, 4)
    for k in range(REACH):
        here = sk.at[k, far]
        remote(here, here, vs.at[k], vr.at[k], sibling).wait_recv()
        go(here, here, ws.at[k, 1], wr.at[k, 1], sibling)
    for dp in range(4):
        for dq in range(4):
            here = block(dp, dq, 1 - c)
            remote(here, here, cs.at[dp, dq], cr.at[dp, dq], sibling).wait_recv()
    near = g + 1 - 2 * c
    for k in range(REACH):
        for side, who in ((0, near), (1, lax.rem(near + 2, 4))):
            here = sk.at[k, who]
            remote(here, here, ws.at[k, side], wr.at[k, side], sibling).wait_recv()
    for copy in sends:
        copy.wait_send()


def gather_keys(prefix_rows, suffix_rows):
    sems = [DMA(()), DMA((8,)), DMA((8,)), DMA((4, 4)), DMA((4, 4)), DMA((4, 4)), DMA((4, 4))]
    sems += [DMA((REACH,))] * 4 + [DMA((REACH, 2))] * 2
    return pl.pallas_call(
        gather_kernel,
        out_shape=(shape((256, PAGE, KEY)), shape((REACH, 4, QUARTER, KEY))),
        in_specs=[ANY, ANY],
        out_specs=(ANY, ANY),
        scratch_shapes=sems,
        compiler_params=params(0),
        name="gather_keys",
    )(prefix_rows, suffix_rows)


def slot_kernel(routes, member, select):
    rows = 2 * QUARTER
    experts = lax.broadcasted_iota(jnp.int32, (rows, EXPERTS), 1)
    hit = jnp.zeros((rows, EXPERTS), F32)
    for k in range(TOP):
        hit = hit + (routes[:, k : k + 1] == experts).astype(F32)
    member[...] = hit
    i = lax.broadcasted_iota(jnp.int32, (rows, rows), 0)
    j = lax.broadcasted_iota(jnp.int32, (rows, rows), 1)
    before = ((j < i) & ((j >> 5) == (i >> 5))).astype(BF16)
    hits = hit.astype(BF16)
    rank = jnp.dot(before, hits, preferred_element_type=F32)
    spread = spread_matrix()
    hit_wide = jnp.dot(hits, spread, preferred_element_type=F32)
    rank_wide = jnp.dot(rank.astype(BF16), spread, preferred_element_type=F32)
    col = lax.broadcasted_iota(jnp.int32, (rows, SLOTS), 1)
    row = lax.broadcasted_iota(jnp.int32, (rows, SLOTS), 0)
    slot = (col & 3).astype(F32)
    chosen = (hit_wide > 0.5) & (rank_wide == slot) & (((col >> 2) & 1) == (row >> 5))
    select[...] = chosen.astype(BF16)


def spread_matrix():
    e = lax.broadcasted_iota(jnp.int32, (EXPERTS, SLOTS), 0)
    col = lax.broadcasted_iota(jnp.int32, (EXPERTS, SLOTS), 1)
    owner = ((col >> 3) & 1) * 32 + (col >> 4)
    return (e == owner).astype(BF16)


def slots(routes_chip):
    return pl.pallas_call(
        slot_kernel,
        out_shape=(shape((64, EXPERTS), F32), shape((64, SLOTS))),
        in_specs=[VM],
        out_specs=(VM, VM),
        compiler_params=params(),
        name="slots",
    )(routes_chip)


def attend_kernel(first_s, lens, tenants, spans, pages, q, ku, vu, ow, pk, sk, own, out, bias, s, acc):
    first = first_s[0]
    r = lax.broadcasted_iota(jnp.int32, (TOK, 1), 0)
    pos = first + (r & 31) * 4 + (r >> 5)

    def one_request(i, state):
        start, begin, low, high = state
        end = start + lens[i]
        inside = (pos >= start) & (pos < end)
        tenant = tenants[i]
        lo = jnp.int32(0)
        for k in range(3):
            lo = lo + jnp.where(k < tenant, spans[k], 0)
        hi = lo + spans[tenant]
        begin = jnp.where(inside, start, begin)
        low = jnp.where(inside, lo, low)
        high = jnp.where(inside, hi, high)
        return end, begin, low, high

    zero = jnp.zeros((TOK, 1), jnp.int32)
    _, begin, low, high = lax.fori_loop(0, 32, one_request, (jnp.int32(0), zero, zero, zero))
    page = lax.broadcasted_iota(jnp.int32, (256, 2048), 0)
    spot = lax.broadcasted_iota(jnp.int32, (256, 2048), 1)
    expand = (page == (spot >> 3)).astype(BF16)
    table = jnp.broadcast_to(pages[...], (8, 256)).astype(F32).astype(BF16)
    logical = jnp.dot(table, expand, preferred_element_type=F32)[0:1].astype(jnp.int32) * PAGE
    logical = logical + (lax.broadcasted_iota(jnp.int32, (1, 2048), 1) & 7)
    seen = (logical >= low) & (logical < high)
    bias[:, 0:2048] = jnp.where(seen, 0.0, VERY_NEGATIVE)
    col = lax.broadcasted_iota(jnp.int32, (1, 640), 1)
    step = col >> 7
    spot = first + (col & 127) - jnp.where(step == 4, 0, (step + 1) * TOK)
    seen = (spot >= begin) & (spot <= pos)
    bias[:, 2048:2688] = jnp.where(seen, 0.0, VERY_NEGATIVE)
    acc[...] = jnp.zeros_like(acc)

    def one_head(h, _):
        qh = q[h]
        absorbed = jnp.dot(qh[:, :NOPE], ku[h], preferred_element_type=F32).astype(BF16)
        full = jnp.concatenate([absorbed, qh[:, NOPE:]], axis=1)
        pieces = ((pk, 0, 2048), (sk, 2048, 2560), (own, 2560, 2688))
        for keys, lo, hi in pieces:
            scores = lax.dot_general(full, keys[...], NT, preferred_element_type=F32)
            s[:, lo:hi] = scores * SCORE_SCALE + bias[:, lo:hi]
        best = jnp.max(s[...], axis=1, keepdims=True)
        total = jnp.zeros((TOK, 1), F32)
        mixed = jnp.zeros((TOK, LAT), F32)
        for keys, lo, hi in pieces:
            weights = jnp.exp(s[:, lo:hi] - best)
            total = total + jnp.sum(weights, axis=1, keepdims=True)
            mixed = mixed + jnp.dot(
                weights.astype(BF16), keys[:, :LAT], preferred_element_type=F32
            )
        latent = (mixed / total).astype(BF16)
        head = jnp.dot(latent, vu[h], preferred_element_type=F32).astype(BF16)
        acc[...] += jnp.dot(head, ow[h], preferred_element_type=F32)
        return 0

    lax.fori_loop(0, HEADS_DEV, one_head, 0)
    out[...] = acc[...].astype(BF16)


def attend(first, lens, tenants, spans, pages, q, ku, vu, ow, pk, sk, own):
    return pl.pallas_call(
        attend_kernel,
        out_shape=shape((TOK, WIDTH)),
        in_specs=[SM, SM, SM, SM] + [VM] * 8,
        out_specs=VM,
        scratch_shapes=[
            pltpu.VMEM((TOK, 2688), F32),
            pltpu.VMEM((TOK, 2688), F32),
            pltpu.VMEM((TOK, WIDTH), F32),
        ],
        compiler_params=params(),
        name="attend",
    )(first, lens, tenants, spans, pages, q, ku, vu, ow, pk, sk, own)


def normalized(values, gain):
    mean_square = jnp.sum(values * values, axis=-1, keepdims=True) * (1.0 / WIDTH)
    return (values * lax.rsqrt(mean_square + NORM_EPSILON) * gain.astype(F32)).astype(BF16)


def reduce_kernel(att, hq, gain, select, packed, resid, rows, near, half, far, both, ns, nr, fs, fr, ts, tr):
    x, y, z, c = coords()
    xh = lax.div(x, 2)
    sibling = device(x, y, z, 1 - c)
    opposite = device(lax.rem(x + 2, 4), y, z, c)
    meet([sibling, opposite])
    to_near = []
    for k in range(2):
        copy = remote(att.at[2 * k + 1 - c], near.at[k], ns.at[k], nr.at[k], sibling)
        copy.start()
        to_near.append(copy)
    for copy in to_near:
        copy.wait()
    half[...] = (att[2 * (1 - xh) + c].astype(F32) + near[1 - xh].astype(F32)).astype(BF16)
    across = remote(half, far, fs, fr, opposite)
    across.start()
    mine = att[2 * xh + c].astype(F32) + near[xh].astype(F32) + hq[...].astype(F32)
    across.wait()
    residual = (mine + far[...].astype(F32)).astype(BF16)
    resid[...] = residual
    both[c] = normalized(residual.astype(F32), gain[...])
    share = remote(both.at[c], both.at[c], ts, tr, sibling)
    share.start()
    share.wait_send()
    remote(both.at[1 - c], both.at[1 - c], ts, tr, sibling).wait_recv()
    rows[...] = both[...].reshape(64, WIDTH)
    part = both[:, :, pl.ds(pl.multiple_of(c * HALF, HALF), HALF)].reshape(64, HALF)
    out = lax.dot_general(select[...], part, TN, preferred_element_type=F32).astype(BF16)
    packed[...] = out.reshape(32, 2, 8, HALF)


def reduce_group(att, hq, gain, select):
    return pl.pallas_call(
        reduce_kernel,
        out_shape=(shape((32, 2, 8, HALF)), shape((QUARTER, WIDTH)), shape((64, WIDTH))),
        in_specs=[VM] * 4,
        out_specs=(VM, VM, VM),
        scratch_shapes=[
            pltpu.VMEM((2, QUARTER, WIDTH), BF16),
            pltpu.VMEM((QUARTER, WIDTH), BF16),
            pltpu.VMEM((QUARTER, WIDTH), BF16),
            pltpu.VMEM((2, QUARTER, WIDTH), BF16),
            DMA((2,)),
            DMA((2,)),
            DMA(()),
            DMA(()),
            DMA(()),
            DMA(()),
        ],
        compiler_params=params(1),
        name="reduce_group",
    )(att, hq, gain, select)


LAG = 4


def dispatch_kernel(packed, rows, land, s1, r1, ls, xs, xr, cs, cr):
    x, y, z, c = coords()
    xl = lax.rem(x, 2)
    here = y * 8 + z
    sibling = device(x, y, z, 1 - c)
    x_dev = [None] + [device(lax.rem(x + d, 4), y, z, c) for d in range(1, 4)]
    barrier = pltpu.get_barrier_semaphore()

    def yz_dev(s):
        return device(x, lax.rem(y + lax.div(s, 8), 4), lax.rem(z + lax.rem(s, 8), 8), c)

    def yz_to(s):
        return lax.rem(y + lax.div(s, 8), 4) * 8 + lax.rem(z + lax.rem(s, 8), 8)

    def yz_from(s):
        return lax.rem(y + 4 - lax.div(s, 8), 4) * 8 + lax.rem(z + 8 - lax.rem(s, 8), 8)

    def greet(s, _):
        pl.semaphore_signal(barrier, inc=1, device_id=yz_dev(s), device_id_type=MESH)
        return 0

    lax.fori_loop(1, 32, greet, 0)
    for peer in x_dev[1:] + [sibling]:
        pl.semaphore_signal(barrier, inc=1, device_id=peer, device_id_type=MESH)
    pl.semaphore_wait(barrier, 35)

    def first_leg(s):
        return remote(packed.at[yz_to(s)], land.at[here], s1.at[s], r1.at[s], yz_dev(s))

    def x_leg(s, d, src):
        spot = rows.at[c, x, yz_from(s)]
        return remote(src, spot, xs.at[d, s], xr.at[d, s], x_dev[d])

    def to_sibling(s, d, src):
        spot = rows.at[c, lax.rem(x + d, 4), yz_from(s)]
        return remote(src, spot, cs.at[d, s], cr, sibling)

    def local(s, src):
        return pltpu.make_async_copy(src, rows.at[c, x, yz_from(s)], ls.at[s])

    def start_first(s, _):
        first_leg(s).start()
        return 0

    lax.fori_loop(1, 32, start_first, 0)
    keep = pltpu.make_async_copy(packed.at[here], land.at[here], s1.at[0])
    keep.start()
    keep.wait()

    def forward(s):
        block = yz_from(s)
        same, other = land.at[block, xl], land.at[block, 1 - xl]
        x_leg(s, 2, same).start()
        x_leg(s, 1, other).start()
        x_leg(s, 3, other).start()
        to_sibling(s, 0, same).start()
        local(s, same).start()

    def pass_on(s):
        for d in (1, 3, 2):
            spot = rows.at[c, lax.rem(x + d, 4), yz_from(s)]
            remote(spot, spot, xs.at[4 - d, s], xr.at[4 - d, s], sibling).wait_recv()
            to_sibling(s, d, spot).start()

    forward(0)

    def step(s, _):
        spot = land.at[yz_from(s)]
        remote(spot, spot, s1.at[s], r1.at[s], sibling).wait_recv()
        forward(s)

        @pl.when(s >= LAG)
        def _():
            pass_on(s - LAG)

        return 0

    lax.fori_loop(1, 32, step, 0)

    def rest(s, _):
        pass_on(s)
        return 0

    lax.fori_loop(32 - LAG, 32, rest, 0)
    remote(rows.at[1 - c], rows.at[1 - c], cs.at[0, 0], cr, sibling).wait_recv()

    def drain(s, _):
        block = yz_from(s)
        same = land.at[block, 0]
        for d in range(1, 4):
            x_leg(s, d, same).wait_send()
        for d in range(4):
            to_sibling(s, d, same).wait_send()
        local(s, same).wait()

        @pl.when(s >= 1)
        def _():
            first_leg(s).wait_send()

        return 0

    lax.fori_loop(0, 32, drain, 0)


def dispatch(packed):
    return pl.pallas_call(
        dispatch_kernel,
        out_shape=shape((2, 4, 32, 8, HALF)),
        in_specs=[ANY],
        out_specs=ANY,
        scratch_shapes=[
            pltpu.VMEM((32, 2, 8, HALF), BF16),
            DMA((32,)),
            DMA((32,)),
            DMA((32,)),
            DMA((4, 32)),
            DMA((4, 32)),
            DMA((4, 32)),
            DMA(()),
        ],
        compiler_params=params(2),
        name="dispatch",
    )(packed)


def split_terms(values, count):
    terms = []
    for _ in range(count):
        term = values.astype(BF16)
        terms.append(term)
        values = values - term.astype(F32)
    return terms


def expert_kernel(rows, gate, up, down, normed, router, member, select, out, mix):
    @pl.when(pl.program_id(0) == 0)
    def _():
        logits = jnp.dot(normed[...], router[...], preferred_element_type=F32)
        picked = jax.nn.sigmoid(logits) * member[...]
        weights = picked / jnp.sum(picked, axis=1, keepdims=True) * ROUTE_SCALING
        spread = spread_matrix()
        wide = jnp.zeros((64, SLOTS), F32)
        for term in split_terms(weights, 3):
            wide = wide + jnp.dot(term, spread, preferred_element_type=F32)
        wide = wide * select[...].astype(F32)
        for k, term in enumerate(split_terms(wide, 2)):
            mix[k] = term

    left, right = rows[0], rows[1]

    def product(weight):
        return jnp.dot(left, weight[:HALF], preferred_element_type=F32) + jnp.dot(
            right, weight[HALF:], preferred_element_type=F32
        )

    gate_vals = product(gate)
    hidden = (gate_vals / (1.0 + jnp.exp(-gate_vals)) * product(up)).astype(BF16)
    result = jnp.dot(hidden, down[...], preferred_element_type=F32).astype(BF16)
    out[0] = result[:, :HALF]
    out[1] = result[:, HALF:]


def experts(rows, gate, up, down, normed, router, member, select):
    chunk = 128
    whole = lambda *dims: pl.BlockSpec(dims, lambda i: (0,) * len(dims))
    moving = pl.BlockSpec((2, chunk, HALF), lambda i: (0, i, 0))
    ff = gate.shape[1]
    return pl.pallas_call(
        expert_kernel,
        out_shape=(shape((2, 1024, HALF)), shape((2, 64, SLOTS))),
        grid=(1024 // chunk,),
        in_specs=[
            moving,
            whole(WIDTH, ff),
            whole(WIDTH, ff),
            whole(ff, WIDTH),
            whole(64, WIDTH),
            whole(WIDTH, EXPERTS),
            whole(64, EXPERTS),
            whole(64, SLOTS),
        ],
        out_specs=(moving, whole(2, 64, SLOTS)),
        compiler_params=params(),
        name="experts",
    )(rows, gate, up, down, normed, router, member, select)


def combine_kernel(
    parts, mix, resid, gain, wq, wl, layer, nq, nl,
    near, summed, landed, turned, back, moe, other, normed,
    ns, nr, xs, xr, bs, br, es, er, hs, hr,
):
    x, y, z, c = coords()
    g = lax.axis_index("group")
    xl = lax.rem(x, 2)
    here = y * 8 + z
    sibling = device(x, y, z, 1 - c)
    x_dev = [None] + [device(lax.rem(x + d, 4), y, z, c) for d in range(1, 4)]
    barrier = pltpu.get_barrier_semaphore()

    def yz_dev(s):
        return device(x, lax.rem(y + lax.div(s, 8), 4), lax.rem(z + lax.rem(s, 8), 8), c)

    def yz_to(s):
        return lax.rem(y + lax.div(s, 8), 4) * 8 + lax.rem(z + lax.rem(s, 8), 8)

    def yz_from(s):
        return lax.rem(y + 4 - lax.div(s, 8), 4) * 8 + lax.rem(z + 8 - lax.rem(s, 8), 8)

    def greet(s, _):
        pl.semaphore_signal(barrier, inc=1, device_id=yz_dev(s), device_id_type=MESH)
        return 0

    lax.fori_loop(1, 32, greet, 0)
    for peer in x_dev[1:] + [sibling]:
        pl.semaphore_signal(barrier, inc=1, device_id=peer, device_id_type=MESH)
    pl.semaphore_wait(barrier, 35)

    def span(j):
        return pl.ds(pl.multiple_of(lax.rem(y + j, 4) * 8, 8), 8)

    order = (2, 1, 3, 0)

    def near_copy(j, d):
        xd = lax.rem(x + d, 4)
        return remote(
            parts.at[1 - c, xd, span(j)], near.at[xd, span(j)], ns.at[j, d], nr.at[j, d], sibling
        )

    def x_copy(j, d):
        xd = lax.rem(x + d, 4)
        return remote(
            summed.at[xd, span(j)], landed.at[d, span(j)], xs.at[j, d], xr.at[j, d], x_dev[d]
        )

    def back_copy(s):
        return remote(turned.at[yz_to(s)], back.at[here], bs.at[s], br.at[s], yz_dev(s))

    def start_near(j, _):
        for d in order:
            near_copy(j, d).start()
        return 0

    lax.fori_loop(0, 4, start_near, 0)

    def sum_near(j, _):
        for d in order:
            near_copy(j, d).wait_recv()
            xd = lax.rem(x + d, 4)
            total = parts[c, xd, span(j)].astype(F32) + near[xd, span(j)].astype(F32)
            summed[xd, span(j)] = total.astype(BF16)
            if d > 0:
                x_copy(j, d).start()
        return 0

    lax.fori_loop(0, 4, sum_near, 0)

    def sum_x(j, _):
        for d in range(1, 4):
            x_copy(j, d).wait_recv()
        same = summed[x, span(j)].astype(F32) + landed[2, span(j)].astype(F32)
        cross = landed[1, span(j)].astype(F32) + landed[3, span(j)].astype(F32)
        turned[span(j), xl] = same.astype(BF16)
        turned[span(j), 1 - xl] = cross.astype(BF16)
        for k in range(8):
            s = j * 8 + k

            @pl.when(s >= 1)
            def _():
                back_copy(s).start()

        return 0

    lax.fori_loop(0, 4, sum_x, 0)
    back[here] = turned[here]

    def arrive(s, _):
        spot = back.at[yz_from(s)]
        remote(spot, spot, bs.at[s], br.at[s], sibling).wait_recv()
        return 0

    lax.fori_loop(1, 32, arrive, 0)
    values = back[...].reshape(SLOTS, HALF)
    gated = jnp.dot(mix[0], values, preferred_element_type=F32)
    gated = gated + jnp.dot(mix[1], values, preferred_element_type=F32)
    moe[...] = gated.reshape(2, QUARTER, HALF)
    swap = remote(moe.at[1 - c], other, es, er, sibling)
    swap.start()
    mine = pl.ds(pl.multiple_of(c * HALF, HALF), HALF)
    theirs = pl.ds(pl.multiple_of((1 - c) * HALF, HALF), HALF)
    layer[:, mine] = (resid[:, mine].astype(F32) + moe[c]).astype(BF16)
    swap.wait()
    layer[:, theirs] = (resid[:, theirs].astype(F32) + other[...]).astype(BF16)
    normed[g] = normalized(layer[...].astype(F32), gain[...])
    gs = g + 1 - 2 * c
    far, far_s = lax.rem(g + 2, 4), lax.rem(gs + 2, 4)

    def share(k, who, dev):
        return remote(normed.at[who], normed.at[who], hs.at[k], hr.at[k], dev)

    def project(who):
        block = normed[who]
        nq[who] = jnp.dot(block, wq[...], preferred_element_type=F32).astype(BF16)
        nl[who] = jnp.dot(block, wl[...], preferred_element_type=F32).astype(BF16)

    share(0, g, x_dev[2]).start()
    share(1, g, sibling).start()
    project(g)
    share(1, gs, sibling).wait_recv()
    project(gs)
    share(0, far, sibling).wait_recv()
    share(2, far, sibling).start()
    project(far)
    share(2, far_s, sibling).wait_recv()
    project(far_s)
    share(0, g, x_dev[2]).wait_send()
    share(1, g, sibling).wait_send()
    share(2, far, sibling).wait_send()

    def drain(j, _):
        for d in order:
            near_copy(j, d).wait_send()
            if d > 0:
                x_copy(j, d).wait_send()
        for k in range(8):
            s = j * 8 + k

            @pl.when(s >= 1)
            def _():
                back_copy(s).wait_send()

        return 0

    lax.fori_loop(0, 4, drain, 0)


def combine(parts, mix, resid, gain, wq, wl):
    cols, lat = wq.shape[1], wl.shape[1]
    return pl.pallas_call(
        combine_kernel,
        out_shape=(
            shape((QUARTER, WIDTH)),
            shape((4, QUARTER, cols)),
            shape((4, QUARTER, lat)),
        ),
        in_specs=[VM] * 6,
        out_specs=(VM, VM, VM),
        scratch_shapes=[
            pltpu.VMEM((4, 32, 8, HALF), BF16),
            pltpu.VMEM((4, 32, 8, HALF), BF16),
            pltpu.VMEM((4, 32, 8, HALF), BF16),
            pltpu.VMEM((32, 2, 8, HALF), BF16),
            pltpu.VMEM((32, 2, 8, HALF), BF16),
            pltpu.VMEM((2, QUARTER, HALF), F32),
            pltpu.VMEM((QUARTER, HALF), F32),
            pltpu.VMEM((4, QUARTER, WIDTH), BF16),
            DMA((4, 4)),
            DMA((4, 4)),
            DMA((4, 4)),
            DMA((4, 4)),
            DMA((32,)),
            DMA((32,)),
            DMA(()),
            DMA(()),
            DMA((3,)),
            DMA((3,)),
        ],
        compiler_params=params(3),
        name="combine",
    )(parts, mix, resid, gain, wq, wl)


def per_device(
    hidden_in,
    queries,
    suffix_latent,
    prefix_latent,
    key_up,
    value_up,
    output_weight,
    norm_gain,
    router,
    expert_gate,
    expert_up,
    expert_down,
    next_gain,
    next_query_weight,
    next_latent_weight,
    suffix_lengths,
    request_tenant,
    tenant_lengths,
    page_table,
    routes,
):
    g = lax.axis_index("group")
    first = (lax.axis_index("tensor") * TOK).astype(jnp.int32).reshape(1)
    pk, sk = gather_keys(prefix_latent, suffix_latent.reshape(4, QUARTER, KEY))
    q = queries.reshape(QUARTER, 4, HEADS_DEV, NOPE + ROPE).transpose(2, 1, 0, 3)
    att = attend(
        first,
        suffix_lengths,
        request_tenant,
        tenant_lengths,
        page_table.reshape(1, -1),
        q.reshape(HEADS_DEV, TOK, NOPE + ROPE),
        key_up,
        value_up,
        output_weight.reshape(HEADS_DEV, NOPE, WIDTH),
        pk.reshape(-1, KEY),
        sk.reshape(-1, KEY),
        suffix_latent,
    )
    chip_routes = lax.dynamic_slice_in_dim(routes, (g // 2) * 2, 2, 0).reshape(64, TOP)
    member, select = slots(chip_routes)
    hq = lax.dynamic_slice_in_dim(hidden_in.reshape(QUARTER, 4, WIDTH), g, 1, 1)
    packed, resid, normed = reduce_group(
        att.reshape(4, QUARTER, WIDTH), hq.reshape(QUARTER, WIDTH), norm_gain.reshape(1, -1), select
    )
    rows = dispatch(packed)
    parts, mix = experts(
        rows.reshape(2, 1024, HALF),
        expert_gate[0],
        expert_up[0],
        expert_down[0],
        normed,
        router,
        member,
        select,
    )
    layer, nq, nl = combine(
        parts.reshape(2, 4, 32, 8, HALF),
        mix,
        resid,
        next_gain.reshape(1, -1),
        next_query_weight,
        next_latent_weight,
    )
    nq = nq.transpose(1, 0, 2).reshape(TOK, -1)
    nl = nl.transpose(1, 0, 2).reshape(TOK, -1)
    return layer.reshape(QUARTER, 1, WIDTH), nq, nl


def solution(mesh):
    return jax.shard_map(
        per_device,
        mesh=mesh,
        in_specs=(
            P("tensor", None),
            P("tensor", "group"),
            P("tensor", None),
            P(("group", "tensor"), None),
            P("group", None, None),
            P("group", None, None),
            P("group", None),
            P(),
            P(),
            P("tensor", None, "group"),
            P("tensor", None, "group"),
            P("tensor", "group", None),
            P(),
            P(None, "group"),
            P(None, "group"),
            P(),
            P(),
            P(),
            P(),
            P(None, "tensor", None),
        ),
        out_specs=(P("tensor", "group", None), P("tensor", "group"), P("tensor", "group")),
        check_vma=False,
    )
```

```python
import math
from types import SimpleNamespace

import jax
import jax.numpy as jnp
from jax import lax
from jax.experimental import pallas as pl
from jax.experimental.pallas import tpu as pltpu
from jax.sharding import PartitionSpec as P

NOPE = 128
ROPE = 64
LAT = 512
KEY = LAT + ROPE
PAGE = 8
REACH = 4
WIDTH = 2048
HALF = WIDTH // 2
EXPERTS = 64
TOP = 6
HEADS_DEV = 4
TOK = 128
QUARTER = 32
SLOTS = EXPERTS * 8
SCORE_SCALE = 1.0 / math.sqrt(NOPE + ROPE)
VERY_NEGATIVE = -1e30
ROUTE_SCALING = 2.446
NORM_EPSILON = 1e-06
BF16 = jnp.bfloat16
F32 = jnp.float32
MESH = pl.DeviceIdType.MESH
ANY = pl.BlockSpec(memory_space=pl.ANY)
VM = pl.BlockSpec(memory_space=pltpu.VMEM)
SM = pl.BlockSpec(memory_space=pltpu.SMEM)
DMA = pltpu.SemaphoreType.DMA
NT = (((1,), (1,)), ((), ()))
TN = (((0,), (0,)), ((), ()))


def coords():
    g = lax.axis_index("group")
    t = lax.axis_index("tensor")
    x = lax.div(g, 2) * 2 + lax.div(t, 32)
    y = lax.rem(lax.div(t, 8), 4)
    z = lax.rem(t, 8)
    return x, y, z, lax.rem(g, 2)


def group_of(x, c):
    return lax.div(x, 2) * 2 + c


def tensor_of(x, y, z):
    return (lax.rem(x, 2) * 4 + y) * 8 + z


def device(x, y, z, c):
    return {"group": group_of(x, c), "tensor": tensor_of(x, y, z)}


def remote(src, dst, send, recv, dev):
    return pltpu.make_async_remote_copy(
        src_ref=src, dst_ref=dst, send_sem=send, recv_sem=recv, device_id=dev, device_id_type=MESH
    )


def meet(peers):
    barrier = pltpu.get_barrier_semaphore()
    for peer in peers:
        pl.semaphore_signal(barrier, inc=1, device_id=peer, device_id_type=MESH)
    pl.semaphore_wait(barrier, len(peers))


def shape(dims, dtype=BF16):
    return jax.ShapeDtypeStruct(dims, dtype)


def iota(dims, axis):
    return lax.broadcasted_iota(jnp.int32, dims, axis)


def dot(a, b, dims=(((1,), (0,)), ((), ()))):
    return lax.dot_general(a, b, dims, preferred_element_type=F32)


def rows_at(start, size):
    return pl.ds(pl.multiple_of(start, size), size)


def normalized(values, gain):
    mean_square = jnp.sum(values * values, axis=-1, keepdims=True) * (1.0 / WIDTH)
    return (values * lax.rsqrt(mean_square + NORM_EPSILON) * gain.astype(F32)).astype(BF16)


def split_terms(values, count):
    terms = []
    for _ in range(count):
        term = values.astype(BF16)
        terms.append(term)
        values = values - term.astype(F32)
    return terms


def token_order():
    i, j = iota((TOK, TOK), 0), iota((TOK, TOK), 1)
    return (j == (i & 31) * 4 + (i >> 5)).astype(BF16)


def slot_spread():
    slot, e = iota((SLOTS, EXPERTS), 0), iota((SLOTS, EXPERTS), 1)
    return (e == ((slot >> 3) & 1) * 32 + (slot >> 4)).astype(BF16)


SPECS = dict(
    lens=SM, tenants=SM, spans=SM, pages=VM, routes=VM, queries=VM, suffix=VM, pref=VM,
    gain=VM, next_gain=VM,
    hidden_h=ANY, ku_h=ANY, vu_h=ANY, ow_h=ANY, gate_h=ANY, up_h=ANY, down_h=ANY,
    router_h=ANY, wq_h=ANY, wl_h=ANY,
)
LOADED = ("ku", "vu", "ow", "hidden", "router", "gate", "up", "down", "wq", "wl")
BLOCK = (8, HALF)
SCRATCH = dict(
    q=pltpu.VMEM((HEADS_DEV, TOK, NOPE + ROPE), BF16),
    ku=pltpu.VMEM((HEADS_DEV, NOPE, LAT), BF16),
    vu=pltpu.VMEM((HEADS_DEV, LAT, NOPE), BF16),
    ow=pltpu.VMEM((HEADS_DEV, NOPE, WIDTH), BF16),
    hidden=pltpu.VMEM((TOK, WIDTH), BF16),
    router=pltpu.VMEM((EXPERTS, WIDTH), BF16),
    gate=pltpu.VMEM((352, WIDTH), BF16),
    up=pltpu.VMEM((352, WIDTH), BF16),
    down=pltpu.VMEM((352, WIDTH), BF16),
    wq=pltpu.VMEM((WIDTH, 768), BF16),
    wl=pltpu.VMEM((144, WIDTH), BF16),
    load_sem=DMA((len(LOADED),)),
    zb=pltpu.VMEM((8, PAGE, KEY), BF16),
    pk=pltpu.VMEM((2048, KEY), BF16),
    sk=pltpu.VMEM((REACH * TOK, KEY), BF16),
    own=pltpu.VMEM((TOK, KEY), BF16),
    zs=DMA((8,)), zr=DMA((8,)),
    bs=DMA((4, 4)), br=DMA((4, 4)), cs=DMA((4, 4)), cr=DMA((4, 4)),
    us=DMA((REACH,)), ur=DMA((REACH,)), vs=DMA((REACH,)), vr=DMA((REACH,)),
    ws=DMA((REACH, 2)), wr=DMA((REACH, 2)),
    bias=pltpu.VMEM((TOK, 2688), F32),
    s=pltpu.VMEM((TOK, 2688), F32),
    acc=pltpu.VMEM((TOK, WIDTH), F32),
    att=pltpu.VMEM((4, QUARTER, WIDTH), BF16),
    near_a=pltpu.VMEM((2, QUARTER, WIDTH), BF16),
    half=pltpu.VMEM((QUARTER, WIDTH), BF16),
    far=pltpu.VMEM((QUARTER, WIDTH), BF16),
    resid=pltpu.VMEM((QUARTER, WIDTH), BF16),
    both=pltpu.VMEM((2, QUARTER, WIDTH), BF16),
    as_=DMA((2,)), ar=DMA((2,)), fs=DMA(()), fr=DMA(()), ts=DMA(()), tr=DMA(()),
    select=pltpu.VMEM((SLOTS, 64), BF16),
    member=pltpu.VMEM((EXPERTS, 64), F32),
    mix=pltpu.VMEM((2, SLOTS, 64), BF16),
    packed=pltpu.VMEM((32, 2) + BLOCK, BF16),
    land=pltpu.VMEM((32, 2) + BLOCK, BF16),
    rows=pltpu.VMEM((2, 4, 32) + BLOCK, BF16),
    parts=pltpu.VMEM((2, 4, 32) + BLOCK, BF16),
    d1s=DMA((32,)), d1r=DMA((32,)), d2s=DMA((4, 32)), d2r=DMA((4, 32)), d3s=DMA((4, 32)), d3r=DMA((4,)),
    near=pltpu.VMEM((4, 32) + BLOCK, BF16),
    summed=pltpu.VMEM((4, 32) + BLOCK, BF16),
    landed=pltpu.VMEM((4, 32) + BLOCK, BF16),
    turned=pltpu.VMEM((32, 2) + BLOCK, BF16),
    back=pltpu.VMEM((32, 2) + BLOCK, BF16),
    e1s=DMA((4, 4)), e1r=DMA((4, 4)), e2s=DMA((4, 4)), e2r=DMA((4, 4)), e3s=DMA((32,)), e3r=DMA((32,)),
    moe=pltpu.VMEM((2, QUARTER, HALF), F32),
    other=pltpu.VMEM((QUARTER, HALF), F32),
    normed=pltpu.VMEM((4, QUARTER, WIDTH), BF16),
    es=DMA(()), er=DMA(()), hs=DMA((3,)), hr=DMA((3,)),
)
OUTS = ("layer", "nq", "nl")


def layer_kernel(*refs):
    r = SimpleNamespace(**dict(zip(tuple(SPECS) + OUTS + tuple(SCRATCH), refs)))
    x, y, z, c = coords()
    g = lax.axis_index("group")
    t = lax.axis_index("tensor")
    xh, xl = lax.div(x, 2), lax.rem(x, 2)
    here = y * 8 + z
    sibling = device(x, y, z, 1 - c)
    x_dev = [None] + [device(lax.rem(x + d, 4), y, z, c) for d in range(1, 4)]
    ahead = [{"group": g, "tensor": lax.rem(t + k, 64)} for k in range(1, REACH + 1)]
    behind = [{"group": g, "tensor": lax.rem(t + 64 - k, 64)} for k in range(1, REACH + 1)]
    barrier = pltpu.get_barrier_semaphore()
    sends = []

    def go(src, dst, send, recv, dev):
        copy = remote(src, dst, send, recv, dev)
        copy.start()
        sends.append(copy)

    def yz(s, sign):
        dy, dz = lax.div(s, 8), lax.rem(s, 8)
        return lax.rem(y + 4 + sign * dy, 4), lax.rem(z + 8 + sign * dz, 8)

    def yz_index(s, sign):
        yy, zz = yz(s, sign)
        return yy * 8 + zz

    def yz_dev(s, sign):
        yy, zz = yz(s, sign)
        return device(x, yy, zz, c)

    def greet(s, _):
        pl.semaphore_signal(barrier, inc=1, device_id=yz_dev(s, 1), device_id_type=MESH)
        return 0

    lax.fori_loop(1, 32, greet, 0)
    peers = x_dev[1:] + [sibling] + ahead + behind
    for peer in peers:
        pl.semaphore_signal(barrier, inc=1, device_id=peer, device_id_type=MESH)
    loads = {}
    for i, name in enumerate(LOADED):
        loads[name] = pltpu.make_async_copy(
            getattr(r, name + "_h"), getattr(r, name), r.load_sem.at[i]
        )
        loads[name].start()
    eye = (iota((TOK, TOK), 0) == iota((TOK, TOK), 1)).astype(BF16)
    r.own[...] = dot(eye, r.suffix[...], NT).astype(BF16)
    r.zb[z] = r.pref[...]
    for h in range(HEADS_DEV):
        r.q[h] = r.queries[:, h * (NOPE + ROPE) : (h + 1) * (NOPE + ROPE)]

    first = t * TOK
    pos = first + iota((TOK, 1), 0)

    def one_request(i, state):
        start, begin, low, high = state
        end = start + r.lens[i]
        inside = (pos >= start) & (pos < end)
        tenant = r.tenants[i]
        lo = jnp.int32(0)
        hi = r.spans[0]
        for k in range(3):
            more = tenant > k
            lo = lo + jnp.where(more, r.spans[k], 0)
            hi = hi + jnp.where(more, r.spans[k + 1], 0)
        begin = jnp.where(inside, start, begin)
        low = jnp.where(inside, lo, low)
        high = jnp.where(inside, hi, high)
        return end, begin, low, high

    zero = jnp.zeros((TOK, 1), jnp.int32)
    _, begin, low, high = lax.fori_loop(0, 32, one_request, (jnp.int32(0), zero, zero, zero))
    page, spot = iota((256, 2048), 0), iota((256, 2048), 1)
    expand = (page == (spot >> 3)).astype(BF16)
    table = jnp.broadcast_to(r.pages[...], (8, 256)).astype(F32).astype(BF16)
    logical = dot(table, expand)[0:1].astype(jnp.int32) * PAGE + (iota((1, 2048), 1) & 7)
    seen = (logical >= low) & (logical < high)
    r.bias[:, 0:2048] = jnp.where(seen, 0.0, VERY_NEGATIVE)
    col = iota((1, 640), 1)
    step = col >> 7
    spot = first + (col & 127) - jnp.where(step == 4, 0, (step + 1) * TOK)
    seen = (spot >= begin) & (spot <= pos)
    r.bias[:, 2048:2688] = jnp.where(seen, 0.0, VERY_NEGATIVE)

    pl.semaphore_wait(barrier, 31 + len(peers))

    z_dev = [None] + [device(x, y, lax.rem(z + d, 8), c) for d in range(1, 8)]
    p_dev = [None] + [
        device(lax.rem(x + d * c, 4), lax.rem(y + d * (1 - c), 4), z, c) for d in range(1, 4)
    ]
    q_dev = [None] + [
        device(lax.rem(x + d * (1 - c), 4), lax.rem(y + d * c, 4), z, c) for d in range(1, 4)
    ]

    def block(dp, dq, core):
        bx = lax.rem(x + 8 - dp * core - dq * (1 - core), 4)
        by = lax.rem(y + 8 - dp * (1 - core) - dq * core, 4)
        return r.pk.at[rows_at((group_of(bx, core) * 64 + tensor_of(bx, by, 0)) * PAGE, 64)]

    def near_rows(k, who):
        return r.sk.at[rows_at((k * 4 + who) * QUARTER, QUARTER)]

    for d in range(1, 8):
        go(r.zb.at[z], r.zb.at[z], r.zs.at[d], r.zr.at[d], z_dev[d])
    for k in range(REACH):
        go(r.own.at[rows_at(g * QUARTER, QUARTER)], near_rows(k, g), r.us.at[k], r.ur.at[k], ahead[k])

    hit = jnp.zeros((EXPERTS, 64), F32)
    for k in range(TOP):
        pair = jnp.where(xh == 0, r.routes[k, 0:2, :], r.routes[k, 2:4, :])
        line = jnp.concatenate([pair[0:1], pair[1:2]], axis=1)
        hit = hit + (line == iota((EXPERTS, 64), 0)).astype(F32)
    r.member[...] = hit
    i, j = iota((64, 64), 0), iota((64, 64), 1)
    before = ((i < j) & ((i >> 5) == (j >> 5))).astype(BF16)
    rank = dot(hit.astype(BF16), before)
    spread = slot_spread()
    hit_wide = dot(spread, hit.astype(BF16))
    rank_wide = dot(spread, rank.astype(BF16))
    slot, token = iota((SLOTS, 64), 0), iota((SLOTS, 64), 1)
    chosen = (hit_wide > 0.5) & (rank_wide == (slot & 3).astype(F32))
    chosen = chosen & (((slot >> 2) & 1) == (token >> 5))
    r.select[...] = chosen.astype(BF16)

    for d in range(1, 8):
        row = r.zb.at[lax.rem(z + 8 - d, 8)]
        remote(row, row, r.zs.at[d], r.zr.at[d], sibling).wait_recv()
    own_rows = rows_at((g * 64 + tensor_of(x, y, 0)) * PAGE, 64)
    r.pk[own_rows] = r.zb[...].reshape(64, KEY)
    start = block(0, 0, c)
    for d in range(1, 4):
        go(start, start, r.bs.at[d, 0], r.br.at[d, 0], p_dev[d])
    for d in range(1, 4):
        go(start, start, r.bs.at[0, d], r.br.at[0, d], q_dev[d])
    go(start, start, r.cs.at[0, 0], r.cr.at[0, 0], sibling)
    for dp in range(1, 4):
        spot = block(dp, 0, c)
        remote(spot, spot, r.bs.at[dp, 0], r.br.at[dp, 0], sibling).wait_recv()
        for d in range(1, 4):
            go(spot, spot, r.bs.at[dp, d], r.br.at[dp, d], q_dev[d])
        go(spot, spot, r.cs.at[dp, 0], r.cr.at[dp, 0], sibling)
    for k in range(REACH):
        spot = near_rows(k, g)
        remote(spot, spot, r.us.at[k], r.ur.at[k], sibling).wait_recv()
        go(spot, spot, r.vs.at[k], r.vr.at[k], x_dev[2])
        go(spot, spot, r.ws.at[k, 0], r.wr.at[k, 0], sibling)
    for dp in range(4):
        for dq in range(1, 4):
            spot = block(dp, dq, c)
            remote(spot, spot, r.bs.at[dp, dq], r.br.at[dp, dq], sibling).wait_recv()
            go(spot, spot, r.cs.at[dp, dq], r.cr.at[dp, dq], sibling)
    far_g = lax.rem(g + 2, 4)
    gs = g + 1 - 2 * c
    far_s = lax.rem(gs + 2, 4)
    for k in range(REACH):
        spot = near_rows(k, far_g)
        remote(spot, spot, r.vs.at[k], r.vr.at[k], sibling).wait_recv()
        go(spot, spot, r.ws.at[k, 1], r.wr.at[k, 1], sibling)
    for dp in range(4):
        for dq in range(4):
            spot = block(dp, dq, 1 - c)
            remote(spot, spot, r.cs.at[dp, dq], r.cr.at[dp, dq], sibling).wait_recv()
    for k in range(REACH):
        for side, who in ((0, gs), (1, far_s)):
            spot = near_rows(k, who)
            remote(spot, spot, r.ws.at[k, side], r.wr.at[k, side], sibling).wait_recv()

    for name in ("ku", "vu", "ow"):
        loads[name].wait()
    r.acc[...] = jnp.zeros_like(r.acc)
    order = token_order()

    def one_head(h, _):
        qh = r.q[h]
        absorbed = dot(qh[:, :NOPE], r.ku[h]).astype(BF16)
        full = jnp.concatenate([absorbed, qh[:, NOPE:]], axis=1)
        pieces = ((r.pk, 0, 2048), (r.sk, 2048, 2560), (r.own, 2560, 2688))
        for keys, lo, hi in pieces:
            r.s[:, lo:hi] = dot(full, keys[...], NT) * SCORE_SCALE + r.bias[:, lo:hi]
        best = jnp.max(r.s[...], axis=1, keepdims=True)
        total = jnp.zeros((TOK, 1), F32)
        mixed = jnp.zeros((TOK, LAT), F32)
        for keys, lo, hi in pieces:
            weights = jnp.exp(r.s[:, lo:hi] - best)
            total = total + jnp.sum(weights, axis=1, keepdims=True)
            mixed = mixed + dot(weights.astype(BF16), keys[:, :LAT])
        latent = (mixed / total).astype(BF16)
        head = dot(latent, r.vu[h]).astype(BF16)
        head = dot(order, head).astype(BF16)
        r.acc[...] += dot(head, r.ow[h])
        return 0

    lax.fori_loop(0, HEADS_DEV, one_head, 0)
    r.att[...] = r.acc[...].astype(BF16).reshape(4, QUARTER, WIDTH)

    for k in range(2):
        go(r.att.at[2 * k + 1 - c], r.near_a.at[k], r.as_.at[k], r.ar.at[k], sibling)
    loads["hidden"].wait()
    mine_rows = (iota((QUARTER, TOK), 1) == iota((QUARTER, TOK), 0) * 4 + g).astype(BF16)
    hq = dot(mine_rows, r.hidden[...])
    for k in range(2):
        remote(r.near_a.at[k], r.near_a.at[k], r.as_.at[k], r.ar.at[k], sibling).wait_recv()
    r.half[...] = (r.att[2 * (1 - xh) + c].astype(F32) + r.near_a[1 - xh].astype(F32)).astype(BF16)
    go(r.half, r.far, r.fs, r.fr, x_dev[2])
    mine = r.att[2 * xh + c].astype(F32) + r.near_a[xh].astype(F32) + hq
    gain = r.gain[...].reshape(1, WIDTH)
    next_gain = r.next_gain[...].reshape(1, WIDTH)
    remote(r.half, r.far, r.fs, r.fr, x_dev[2]).wait_recv()
    residual = (mine + r.far[...].astype(F32)).astype(BF16)
    r.resid[...] = residual
    r.both[c] = normalized(residual.astype(F32), gain)
    go(r.both.at[c], r.both.at[c], r.ts, r.tr, sibling)
    remote(r.both.at[1 - c], r.both.at[1 - c], r.ts, r.tr, sibling).wait_recv()
    part = r.both[:, :, rows_at(c * HALF, HALF)].reshape(64, HALF)
    r.packed[...] = dot(r.select[...], part).astype(BF16).reshape((32, 2) + BLOCK)

    def first_leg(s):
        return remote(r.packed.at[yz_index(s, 1)], r.land.at[here], r.d1s.at[s], r.d1r.at[s], yz_dev(s, 1))

    def x_leg(s, d, src):
        spot = r.rows.at[c, x, yz_index(s, -1)]
        return remote(src, spot, r.d2s.at[d, s], r.d2r.at[d, s], x_dev[d])

    def to_sibling(s, d, src):
        spot = r.rows.at[c, lax.rem(x + d, 4), yz_index(s, -1)]
        return remote(src, spot, r.d3s.at[d, s], r.d3r.at[lax.div(s, 8)], sibling)

    def start_first(s, _):
        first_leg(s).start()
        return 0

    lax.fori_loop(1, 32, start_first, 0)
    r.land[here] = r.packed[here]

    def forward(s, _):
        block = yz_index(s, -1)

        @pl.when(s >= 1)
        def _():
            spot = r.land.at[block]
            remote(spot, spot, r.d1s.at[s], r.d1r.at[s], sibling).wait_recv()

        same, cross = r.land.at[block, xl], r.land.at[block, 1 - xl]
        x_leg(s, 2, same).start()
        x_leg(s, 1, cross).start()
        x_leg(s, 3, cross).start()
        to_sibling(s, 0, same).start()
        r.rows[c, x, block] = r.land[block, xl]
        return 0

    def pass_on(s, _):
        for d in (1, 3, 2):
            spot = r.rows.at[c, lax.rem(x + d, 4), yz_index(s, -1)]
            remote(spot, spot, r.d2s.at[4 - d, s], r.d2r.at[4 - d, s], sibling).wait_recv()
            to_sibling(s, d, spot).start()
        return 0

    def span(k):
        return rows_at(lax.rem(y + 4 - k, 4) * 8, 8)

    def near_copy(k, d):
        xd = lax.rem(x + d, 4)
        return remote(
            r.parts.at[1 - c, xd, span(k)], r.near.at[xd, span(k)], r.e1s.at[k, d], r.e1r.at[k, d], sibling
        )

    def x_copy(k, d):
        xd = lax.rem(x + d, 4)
        return remote(
            r.summed.at[xd, span(k)], r.landed.at[d, span(k)], r.e2s.at[k, d], r.e2r.at[k, d], x_dev[d]
        )

    def back_copy(s):
        return remote(r.turned.at[yz_index(s, -1)], r.back.at[here], r.e3s.at[s], r.e3r.at[s], yz_dev(s, -1))

    turn_order = (2, 1, 3, 0)

    def expert(k):
        spot = r.rows.at[1 - c, :, span(k)]
        remote(spot, spot, r.d3s.at[0, 0], r.d3r.at[k], sibling).wait_recv()
        left = r.rows[0, :, span(k)].reshape(256, HALF)
        right = r.rows[1, :, span(k)].reshape(256, HALF)
        gate_vals = dot(left, r.gate[:, :HALF], NT) + dot(right, r.gate[:, HALF:], NT)
        up_vals = dot(left, r.up[:, :HALF], NT) + dot(right, r.up[:, HALF:], NT)
        hidden = (gate_vals / (1.0 + jnp.exp(-gate_vals)) * up_vals).astype(BF16)
        for side in range(2):
            result = dot(hidden, r.down[:, side * HALF : (side + 1) * HALF]).astype(BF16)
            r.parts[side, :, span(k)] = result.reshape((4, 8) + BLOCK)
        for d in turn_order:
            near_copy(k, d).start()

    def sum_near(k):
        for d in turn_order:
            near_copy(k, d).wait_recv()
            xd = lax.rem(x + d, 4)
            total = r.parts[c, xd, span(k)].astype(F32) + r.near[xd, span(k)].astype(F32)
            r.summed[xd, span(k)] = total.astype(BF16)
            if d > 0:
                x_copy(k, d).start()

    loads["router"].wait()
    logits = dot(r.router[...], r.both[...].reshape(64, WIDTH), NT)
    picked = jax.nn.sigmoid(logits) * r.member[...]
    weights = picked / jnp.sum(picked, axis=0, keepdims=True) * ROUTE_SCALING
    wide = jnp.zeros((SLOTS, 64), F32)
    spread = slot_spread()
    for term in split_terms(weights, 3):
        wide = wide + dot(spread, term)
    wide = wide * r.select[...].astype(F32)
    for k, term in enumerate(split_terms(wide, 2)):
        r.mix[k] = term
    for name in ("gate", "up", "down"):
        loads[name].wait()

    def stage(k, _):
        lax.fori_loop(k * 8, k * 8 + 8, forward, 0)

        @pl.when(k >= 2)
        def _():
            expert(k - 2)

        @pl.when(k >= 3)
        def _():
            sum_near(k - 3)

        @pl.when(k >= 1)
        def _():
            lax.fori_loop(k * 8 - 8, k * 8, pass_on, 0)

        return 0

    lax.fori_loop(0, 4, stage, 0)

    def late(k, _):
        expert(k)
        sum_near(k - 1)

        @pl.when(k == 2)
        def _():
            lax.fori_loop(24, 32, pass_on, 0)

        return 0

    lax.fori_loop(2, 4, late, 0)
    sum_near(3)

    def sum_x(k, _):
        for d in range(1, 4):
            x_copy(k, d).wait_recv()
        same = r.summed[x, span(k)].astype(F32) + r.landed[2, span(k)].astype(F32)
        cross = r.landed[1, span(k)].astype(F32) + r.landed[3, span(k)].astype(F32)
        r.turned[span(k), xl] = same.astype(BF16)
        r.turned[span(k), 1 - xl] = cross.astype(BF16)
        for n in range(8):
            s = k * 8 + n

            @pl.when(s >= 1)
            def _():
                back_copy(s).start()

        return 0

    lax.fori_loop(0, 4, sum_x, 0)
    r.back[here] = r.turned[here]

    def arrive(s, _):
        spot = r.back.at[yz_index(s, 1)]
        remote(spot, spot, r.e3s.at[s], r.e3r.at[s], sibling).wait_recv()
        return 0

    lax.fori_loop(1, 32, arrive, 0)
    values = r.back[...].reshape(SLOTS, HALF)
    gated = dot(r.mix[0], values, TN) + dot(r.mix[1], values, TN)
    r.moe[...] = gated.reshape(2, QUARTER, HALF)
    go(r.moe.at[1 - c], r.other, r.es, r.er, sibling)
    my_cols, their_cols = rows_at(c * HALF, HALF), rows_at((1 - c) * HALF, HALF)
    r.layer[:, my_cols] = (r.resid[:, my_cols].astype(F32) + r.moe[c]).astype(BF16)
    remote(r.moe.at[1 - c], r.other, r.es, r.er, sibling).wait_recv()
    r.layer[:, their_cols] = (r.resid[:, their_cols].astype(F32) + r.other[...]).astype(BF16)
    r.normed[g] = normalized(r.layer[...].astype(F32), next_gain)

    def share(k, who, dev):
        return remote(r.normed.at[who], r.normed.at[who], r.hs.at[k], r.hr.at[k], dev)

    share(0, g, x_dev[2]).start()
    share(1, g, sibling).start()
    loads["wq"].wait()
    loads["wl"].wait()
    share(0, far_g, sibling).wait_recv()
    share(2, far_g, sibling).start()
    share(1, gs, sibling).wait_recv()
    share(2, far_s, sibling).wait_recv()
    block = dot(order, r.normed[...].reshape(TOK, WIDTH), TN).astype(BF16)
    r.nq[...] = dot(block, r.wq[...]).astype(BF16)
    r.nl[...] = dot(r.wl[...], block, NT).astype(BF16)

    for copy in sends:
        copy.wait_send()
    share(0, g, x_dev[2]).wait_send()
    share(1, g, sibling).wait_send()
    share(2, far_g, sibling).wait_send()

    def drain(s, _):
        for d in range(1, 4):
            x_leg(s, d, r.land.at[0, 0]).wait_send()
        for d in range(4):
            to_sibling(s, d, r.land.at[0, 0]).wait_send()

        @pl.when(s >= 1)
        def _():
            first_leg(s).wait_send()
            back_copy(s).wait_send()

        return 0

    lax.fori_loop(0, 32, drain, 0)

    def drain_chunks(k, _):
        for d in turn_order:
            near_copy(k, d).wait_send()
            if d > 0:
                x_copy(k, d).wait_send()
        return 0

    lax.fori_loop(0, 4, drain_chunks, 0)


def whole_layer(**operands):
    return pl.pallas_call(
        layer_kernel,
        out_shape=(shape((QUARTER, WIDTH)), shape((TOK, 768)), shape((144, TOK))),
        in_specs=list(SPECS.values()),
        out_specs=(VM, VM, VM),
        scratch_shapes=list(SCRATCH.values()),
        compiler_params=pltpu.CompilerParams(
            collective_id=0, has_side_effects=True, vmem_limit_bytes=60 << 20
        ),
        name="layer",
    )(*[operands[name] for name in SPECS])


def per_device(
    hidden_in,
    queries,
    suffix_latent,
    prefix_latent,
    key_up,
    value_up,
    output_weight,
    norm_gain,
    router,
    expert_gate,
    expert_up,
    expert_down,
    next_gain,
    next_query_weight,
    next_latent_weight,
    suffix_lengths,
    request_tenant,
    tenant_lengths,
    page_table,
    routes,
):
    layer, nq, nl = whole_layer(
        lens=suffix_lengths,
        tenants=request_tenant,
        spans=tenant_lengths,
        pages=page_table.reshape(1, -1),
        routes=routes.transpose(2, 0, 1),
        queries=queries,
        suffix=suffix_latent.T,
        pref=prefix_latent,
        gain=norm_gain,
        next_gain=next_gain,
        hidden_h=hidden_in,
        ku_h=key_up,
        vu_h=value_up,
        ow_h=output_weight.reshape(HEADS_DEV, NOPE, WIDTH),
        gate_h=expert_gate[0].T,
        up_h=expert_up[0].T,
        down_h=expert_down[0],
        router_h=router.T,
        wq_h=next_query_weight,
        wl_h=next_latent_weight.T,
    )
    return layer.reshape(QUARTER, 1, WIDTH), nq, nl.T


def solution(mesh):
    return jax.shard_map(
        per_device,
        mesh=mesh,
        in_specs=(
            P("tensor", None),
            P("tensor", "group"),
            P("tensor", None),
            P(("group", "tensor"), None),
            P("group", None, None),
            P("group", None, None),
            P("group", None),
            P(),
            P(),
            P("tensor", None, "group"),
            P("tensor", None, "group"),
            P("tensor", "group", None),
            P(),
            P(None, "group"),
            P(None, "group"),
            P(),
            P(),
            P(),
            P(),
            P(None, "tensor", None),
        ),
        out_specs=(P("tensor", "group", None), P("tensor", "group"), P("tensor", "group")),
        check_vma=False,
    )
```
